256 devices in a mesh: expert: 8 (over x, core), dp: 32 (over z, y).
Axes of the slice: x: 4, y: 4, z: 8, core: 2. Of those that a mesh axis runs over, the one named last changes fastest.
Arguments:
- tokens: bfloat16 [32768, 2048], P(('expert', 'dp')), may hold values from -24 to 24
- routes: int32 [32768, 2], P(('expert', 'dp')), may hold values from 0 to 7, all different within a row; in each aligned block of 128 rows (0 to 127, 128 to 255, ...) at most 48 rows name the same one
- gate_code: int32 [32768, 2], P(('expert', 'dp')), may hold values from 16 to 128
- w_gate: bfloat16 [8, 2048, 768], P('expert'), may hold values from -0.125 to 0.125
- w_up: bfloat16 [8, 2048, 768], P('expert'), may hold values from -0.125 to 0.125
- w_down: bfloat16 [8, 768, 2048], P('expert'), may hold values from -0.21875 to 0.21875
- grad_out: bfloat16 [32768, 2048], P(('expert', 'dp')), may hold values from -6 to 6
Outputs:
- mixed: bfloat16 [32768, 2048], P(('expert', 'dp'))
- token_grad: bfloat16 [32768, 2048], P(('expert', 'dp'))
- grad_gate: float32 [8, 2048, 768], P('expert', 'dp')
- grad_up: float32 [8, 2048, 768], P('expert', 'dp')
- grad_down: float32 [8, 768, 2048], P('expert', 'dp')
The draws below stay inside these ranges and needn't reach their ends.
Inputs may be any that keep to these rules, and one draw needn't show every extreme that they name: `routes`: each row names 2 different experts; within the rows of one device no expert is named by more than 48 rows, and in every draw some expert is named by exactly 48 rows of some device.
All inputs are finite; a program needn't handle non-finite values.
Results may differ from the reference program's by a relative error of at most 0.015.
Values may be sent and summed in bfloat16 or wider, within the bound.
No kernel may reach another device: no remote copies, remote signals or barrier semaphores. Data moves between devices by JAX's collectives and lax.ppermute only.
A program may use at most 128 MiB of HBM per device.

```python
import math
import jax
import jax.numpy as jnp
import numpy as np
from jax import lax

D = 2048
H = 768
TOP = 2
TOK_DEV = 128
EXPERTS = 8
CAP = 48
TOKENS = 32768
N_EXPERT = 8
N_DP = 32


def set_ends(entries, own_key, smallest, top_value):
    shape = entries.shape
    index_at = [jax.random.randint(jax.random.fold_in(own_key, axis), (), 0, shape[axis]) for axis in range(len(shape))]
    entries = entries.at[tuple(index_at)].set(smallest)
    longest = shape.index(max(shape))
    index_at[longest] = (index_at[longest] + 1) % shape[longest]
    return entries.at[tuple(index_at)].set(top_value)


def spiked(array, stream_key, source, target, blocks, factor):
    def block_of(position):
        return (jnp.arange(array.shape[position]) // (array.shape[position] // blocks)).reshape((-1,) + (1,) * (array.ndim - 1 - position))

    first = jax.random.permutation(stream_key, blocks)[block_of(target)]
    second = (block_of(target) + blocks // 2) % blocks
    return jnp.where((block_of(source) == first) | (block_of(source) == second), factor * array, array)


def steps_of(own_key, extent, split, low, top_value):
    loudness = 1.0
    for dim, parts in split:
        draws = jax.random.uniform(jax.random.fold_in(jax.random.fold_in(own_key, 6), dim), (parts,), jnp.float32, low / len(split), top_value / len(split))
        loudness = loudness * jnp.repeat(jnp.exp(draws), extent[dim] // parts).reshape((-1,) + (1,) * (len(extent) - 1 - dim))
    return loudness


def shared_out(stream_key, own, number, rows, count, top, limit, lean):
    ranking = jax.random.permutation(stream_key, count)
    packed, usual = portions_of(count, rows * top, limit, lean, True), portions_of(count, rows * top, limit, lean, False)
    places = jnp.arange(count)

    def named(lengths, turn):
        used = int((lengths > 0).sum())
        fixed = max(1, used // 4)
        moved = fixed + (places - fixed + turn * (used - fixed)) % max(1, count - fixed)
        return jnp.zeros((count,), jnp.int32).at[ranking[jnp.where(places < fixed, places, moved)]].set(jnp.asarray(lengths, jnp.int32))

    lengths = jnp.where(number % 4 == 0, named(packed, number // 4), named(usual, number - number // 4 - 1))
    mixed = jax.random.permutation(jax.random.fold_in(own, 3), count)
    donor, taker = mixed[0:count // 2 * 2:2], mixed[1:count // 2 * 2:2]
    room = jnp.minimum(lengths[donor] - 1, limit - lengths[taker]) // 2
    room = jnp.where((donor == ranking[0]) | (taker == ranking[0]) | (lengths[taker] == 0), 0, jnp.maximum(room, 0))
    moved = jax.random.randint(jax.random.fold_in(own, 4), (count // 2,), 0, 1 << 20) % (room + 1)
    lengths = lengths.at[donor].add(-moved).at[taker].add(moved)
    items = jnp.searchsorted(jnp.cumsum(lengths), jnp.arange(rows * top), side="right").astype(jnp.int32)
    listing = items.reshape(top, rows).T
    listing = listing[jax.random.permutation(jax.random.fold_in(own, 1), rows)]
    turn = jax.random.randint(jax.random.fold_in(own, 2), (rows, 1), 0, top)
    return jnp.take_along_axis(listing, (jnp.arange(top)[None, :] + turn) % top, axis=1)


def portions_of(count, total, reach, skew, full):
    portions = [(1 << 20) // math.isqrt(standing ** skew) + 1 for standing in range(1, count + 1)]
    largest = reach if full else min(reach, max(-(-total // count), total * portions[0] // sum(portions)))
    least = 1 if total - largest >= count - 1 else 0
    given, surplus = [largest] + [least] * (count - 1), total - largest - least * (count - 1)
    while surplus > 0:
        candidates = [i for i in range(1, count) if given[i] < largest] or [i for i in range(1, count) if given[i] < reach]
        mass, remaining = sum([portions[i] for i in candidates]), surplus
        for i in candidates:
            extra = min(reach - given[i], max(1, remaining * portions[i] // mass), surplus)
            given[i] = given[i] + extra
            surplus = surplus - extra
    return np.array(given)


def scatter_about(stream_key, shape, scale, bound, split=(), kind=jnp.bfloat16):
    loudness = steps_of(stream_key, shape, split, -0.22, 0.18) if split else 1.0
    entries = jax.random.normal(stream_key, shape, jnp.float32) * scale * loudness
    return jnp.minimum(jnp.maximum(entries, -bound), bound).astype(kind)


def gaussian_with(own_key, dims, width, bound, split, heavy, kind=jnp.bfloat16):
    result = width * jax.random.normal(own_key, dims, jnp.float32)
    if split:
        result = result * steps_of(own_key, dims, split, -0.22, 0.18)
    return jnp.clip(spiked(result, jax.random.fold_in(own_key, 3), *heavy), -bound, bound).astype(kind)


def setup_inputs(seed: int = 0) -> dict:
    arg_keys = jax.random.split(jax.random.key(seed), 8)
    tokens = gaussian_with(arg_keys[0], (TOKENS, D), 1.0, 24.0, ((0, 256),), (0, 1, 256, 6.0))
    routes_keys = jax.random.split(jax.random.fold_in(arg_keys[1], 1), TOKENS // TOK_DEV)
    routes_turns = jax.random.permutation(jax.random.fold_in(arg_keys[1], 3), TOKENS // TOK_DEV)
    routes = jax.vmap(lambda own, number: shared_out(jax.random.fold_in(arg_keys[1], 2), own, number, TOK_DEV, EXPERTS, TOP, CAP, 2))(routes_keys, routes_turns).reshape((TOKENS, TOP))
    gate_code = set_ends(jax.random.randint(arg_keys[2], (TOKENS, TOP), 16, 129), jax.random.fold_in(arg_keys[2], 1), 16, 128).astype(jnp.int32)
    w_gate = scatter_about(arg_keys[3], (EXPERTS, D, H), D ** -0.5, 0.125, ((0, 8),))
    w_up = scatter_about(arg_keys[4], (EXPERTS, D, H), D ** -0.5, 0.125, ((0, 8),))
    w_down = scatter_about(arg_keys[5], (EXPERTS, H, D), H ** -0.5, 0.21875, ((0, 8),))
    grad_out = scatter_about(arg_keys[6], (TOKENS, D), 1.0, 6.0, ((0, 256),))
    return dict(tokens=tokens, routes=routes, gate_code=gate_code, w_gate=w_gate, w_up=w_up, w_down=w_down, grad_out=grad_out)


def slot_targets(route_ids):
    flat_ids = route_ids.reshape(-1)
    onehot = (flat_ids[:, None] == jnp.arange(EXPERTS, dtype=jnp.int32)[None, :]).astype(jnp.int32)
    before = jnp.cumsum(onehot, axis=0) - onehot
    slot_of = jnp.sum(before * onehot, axis=1)
    return (flat_ids * CAP + slot_of).reshape(route_ids.shape).astype(jnp.int32)


def scatter_rows(values, targets):
    buffer = jnp.zeros((EXPERTS * CAP, D), values.dtype)
    return buffer.at[targets.reshape(-1)].set(values.reshape(-1, D))


def pick_rows(buffer, targets):
    return buffer[targets]


def to_experts(sent):
    shaped = sent.reshape(N_EXPERT, N_DP, EXPERTS, CAP, D)
    return jnp.transpose(shaped, (2, 1, 0, 3, 4)).reshape(EXPERTS, N_DP, N_EXPERT * CAP, D)


def from_experts(finished):
    shaped = finished.reshape(EXPERTS, N_DP, N_EXPERT, CAP, D)
    return jnp.transpose(shaped, (2, 1, 0, 3, 4)).reshape(N_EXPERT * N_DP, EXPERTS * CAP, D)


def rounded_sum(partial_value):
    narrow = lax.optimization_barrier(partial_value.astype(jnp.bfloat16))
    return jnp.sum(narrow.astype(jnp.float32), axis=0)


def expert_pass(operands):
    rows, grad_rows, weight_gate, weight_up, weight_down = operands
    x_rows = rows.astype(jnp.float32)
    dy_rows = grad_rows.astype(jnp.float32)
    gate_wide = weight_gate.astype(jnp.float32)
    up_wide = weight_up.astype(jnp.float32)
    down_wide = weight_down.astype(jnp.float32)
    pre_gate = jnp.einsum("nrd,dh->nrh", x_rows, gate_wide)
    pre_up = jnp.einsum("nrd,dh->nrh", x_rows, up_wide)
    sigmoid_gate = jax.nn.sigmoid(pre_gate)
    swished = pre_gate * sigmoid_gate
    hidden = (swished * pre_up).astype(jnp.bfloat16)
    hidden_wide = hidden.astype(jnp.float32)
    outputs = jnp.einsum("nrh,hd->nrd", hidden_wide, down_wide).astype(jnp.bfloat16)
    d_hidden = jnp.einsum("nrd,hd->nrh", dy_rows, down_wide)
    d_gate = (d_hidden * pre_up * sigmoid_gate * (1.0 + pre_gate * (1.0 - sigmoid_gate))).astype(jnp.bfloat16)
    d_up = (d_hidden * swished).astype(jnp.bfloat16)
    d_gate_wide = d_gate.astype(jnp.float32)
    d_up_wide = d_up.astype(jnp.float32)
    d_rows = (jnp.einsum("nrh,dh->nrd", d_gate_wide, gate_wide) + jnp.einsum("nrh,dh->nrd", d_up_wide, up_wide)).astype(jnp.bfloat16)
    grad_gate = rounded_sum(jnp.einsum("nrd,nrh->ndh", x_rows, d_gate_wide))
    grad_up = rounded_sum(jnp.einsum("nrd,nrh->ndh", x_rows, d_up_wide))
    grad_down = rounded_sum(jnp.einsum("nrh,nrd->nhd", hidden_wide, dy_rows))
    return outputs, d_rows, grad_gate, grad_up, grad_down


def reference(tokens, routes, gate_code, w_gate, w_up, w_down, grad_out):
    devices = N_EXPERT * N_DP
    targets = jax.vmap(slot_targets)(routes.reshape(devices, TOK_DEV, TOP))
    gates = gate_code.reshape(devices, TOK_DEV, TOP).astype(jnp.float32) / 128.0
    token_rows = jnp.broadcast_to(tokens.reshape(devices, TOK_DEV, 1, D), (devices, TOK_DEV, TOP, D))
    scaled = (gates[..., None] * grad_out.reshape(devices, TOK_DEV, 1, D).astype(jnp.float32)).astype(jnp.bfloat16)
    sent_tokens = jax.vmap(scatter_rows)(token_rows, targets)
    sent_grads = jax.vmap(scatter_rows)(scaled, targets)
    outputs, d_rows, grad_gate, grad_up, grad_down = lax.map(expert_pass, (to_experts(sent_tokens), to_experts(sent_grads), w_gate, w_up, w_down))
    back_out = from_experts(outputs)
    back_grad = from_experts(d_rows)
    picked = jax.vmap(pick_rows)(back_out, targets).astype(jnp.float32)
    mixed = jnp.sum(gates[..., None] * picked, axis=2).astype(jnp.bfloat16).reshape(TOKENS, D)
    picked_grad = jax.vmap(pick_rows)(back_grad, targets).astype(jnp.float32)
    token_grad = jnp.sum(picked_grad, axis=2).astype(jnp.bfloat16).reshape(TOKENS, D)
    return mixed, token_grad, grad_gate, grad_up, grad_down
```

```python
import jax
import jax.numpy as jnp
from jax import lax
from jax.sharding import Mesh
from jax.sharding import PartitionSpec as P

TOP = 2
EXPERT = ("x", "core")
DP = ("z", "y")
ALL = EXPERT + DP


def shift(value, axis, by):
    n = lax.axis_size(axis)
    return lax.ppermute(value, axis, [(i, (i + by) % n) for i in range(n)])


def add(left, right):
    return (left.astype(jnp.float32) + right.astype(jnp.float32)).astype(jnp.bfloat16)


def ring_sum(parts, axis, dim):
    n = lax.axis_size(axis)
    me = lax.axis_index(axis)
    half = n // 2
    other = 1 - dim
    mid = parts.shape[other] // 2

    def piece(step):
        return lax.dynamic_slice_in_dim(parts, (me + step) % n, 1, dim)

    def front(value):
        return lax.slice_in_dim(value, 0, mid, axis=other)

    def back(value):
        return lax.slice_in_dim(value, mid, None, axis=other)

    far = piece(half)
    right, left = shift(front(far), axis, 1), shift(back(far), axis, -1)
    for step in range(half - 1, 0, -1):
        ahead, behind = piece(step), piece(-step)
        if step == half - 1:
            ahead = jnp.concatenate([add(front(ahead), right), back(ahead)], axis=other)
            behind = jnp.concatenate([front(behind), add(back(behind), left)], axis=other)
        else:
            ahead, behind = add(ahead, right), add(behind, left)
        right, left = shift(ahead, axis, 1), shift(behind, axis, -1)
    total = piece(0).astype(jnp.float32) + right.astype(jnp.float32) + left.astype(jnp.float32)
    return jnp.squeeze(total, dim)


def exchange_sum(parts, axis):
    arrived = lax.all_to_all(parts, axis, split_axis=0, concat_axis=0, tiled=True)
    return arrived.astype(jnp.float32).sum(axis=0)


def route_rows(buffer, experts):
    pieces = buffer.reshape(experts, -1, buffer.shape[1])
    return lax.all_to_all(pieces, EXPERT, split_axis=0, concat_axis=0, tiled=True).reshape(
        buffer.shape
    )


def contract_rows(left, right):
    return lax.dot_general(
        left, right, (((0,), (0,)), ((), ())), preferred_element_type=jnp.float32
    )


def contract_last(left, right):
    return lax.dot_general(
        left, right, (((1,), (1,)), ((), ())), preferred_element_type=jnp.float32
    )


def grid(share):
    z, y = lax.axis_size("z"), lax.axis_size("y")
    return share.reshape(z, y, -1, share.shape[1])


def y_first(share):
    part = ring_sum(grid(share), "y", 1).astype(jnp.bfloat16)
    return exchange_sum(part, "z")


def z_first(share):
    part = ring_sum(grid(share), "z", 0).astype(jnp.bfloat16)
    return exchange_sum(part, "y")


def local(tokens, routes, gate_code, w_gate, w_up, w_down, grad_out):
    experts = lax.axis_size(EXPERT)
    tok_rows = tokens.shape[0]
    capacity = (tok_rows * TOP * 3 // (2 * experts) + 7) // 8 * 8
    ids = routes.T
    gates = gate_code.T.astype(jnp.float32) / 128.0
    names = lax.broadcasted_iota(jnp.int32, (experts, tok_rows), 0)
    hits = [(ids[k][None, :] == names).astype(jnp.float32) for k in range(TOP)]
    earlier = (
        lax.broadcasted_iota(jnp.int32, (tok_rows, tok_rows), 0)
        < lax.broadcasted_iota(jnp.int32, (tok_rows, tok_rows), 1)
    ).astype(jnp.bfloat16)
    before = jnp.dot(
        sum(hits).astype(jnp.bfloat16), earlier, preferred_element_type=jnp.float32
    )
    places = lax.broadcasted_iota(jnp.int32, (experts * capacity, tok_rows), 0)
    select = jnp.zeros((experts * capacity, tok_rows), jnp.float32)
    weighted = select
    for k in range(TOP):
        slot = jnp.sum(before * hits[k], axis=0).astype(jnp.int32)
        match = places == (ids[k] * capacity + slot)[None, :]
        select = select + match.astype(jnp.float32)
        weighted = weighted + jnp.where(match, gates[k][None, :], 0.0)
    select, weighted = select.astype(jnp.bfloat16), weighted.astype(jnp.bfloat16)
    sent_tokens = jnp.dot(select, tokens, preferred_element_type=jnp.float32).astype(jnp.bfloat16)
    sent_grads = jnp.dot(weighted, grad_out, preferred_element_type=jnp.float32).astype(
        jnp.bfloat16
    )
    rows = route_rows(sent_tokens, experts)
    rows, sent_grads = lax.optimization_barrier((rows, sent_grads))
    grad_rows = route_rows(sent_grads, experts)
    weight_gate, weight_up, weight_down = w_gate[0], w_up[0], w_down[0]
    pre_gate = jnp.dot(rows, weight_gate, preferred_element_type=jnp.float32)
    pre_up = jnp.dot(rows, weight_up, preferred_element_type=jnp.float32)
    sigmoid_gate = jax.nn.sigmoid(pre_gate)
    swished = pre_gate * sigmoid_gate
    hidden = (swished * pre_up).astype(jnp.bfloat16)
    outputs = jnp.dot(hidden, weight_down, preferred_element_type=jnp.float32).astype(jnp.bfloat16)
    grad_rows, outputs = lax.optimization_barrier((grad_rows, outputs))
    share_down = y_first(contract_rows(hidden, grad_rows).astype(jnp.bfloat16))
    returned = route_rows(outputs, experts)
    d_hidden = contract_last(grad_rows, weight_down)
    d_gate = (d_hidden * pre_up * sigmoid_gate * (1.0 + pre_gate * (1.0 - sigmoid_gate))).astype(
        jnp.bfloat16
    )
    d_up = (d_hidden * swished).astype(jnp.bfloat16)
    share_up = z_first(contract_rows(rows, d_up).astype(jnp.bfloat16))
    share_gate = y_first(contract_rows(rows, d_gate).astype(jnp.bfloat16))
    d_rows = (contract_last(d_gate, weight_gate) + contract_last(d_up, weight_up)).astype(
        jnp.bfloat16
    )
    back_grad = route_rows(d_rows, experts)
    mixed = contract_rows(weighted, returned).astype(jnp.bfloat16)
    token_grad = contract_rows(select, back_grad).astype(jnp.bfloat16)
    return (mixed, token_grad, share_gate[None], share_up[None], share_down[None])


def solution(mesh):
    torus = Mesh(mesh.devices.reshape(4, 2, 8, 4), ALL)
    in_specs = (
        P(ALL, None),
        P(ALL, None),
        P(ALL, None),
        P(EXPERT, None, None),
        P(EXPERT, None, None),
        P(EXPERT, None, None),
        P(ALL, None),
    )
    out_specs = (
        P(ALL, None),
        P(ALL, None),
        P(EXPERT, DP, None),
        P(EXPERT, DP, None),
        P(EXPERT, DP, None),
    )
    return jax.shard_map(local, mesh=torus, in_specs=in_specs, out_specs=out_specs, check_vma=False)
```
